32 devices in a mesh: dp: 16 (over z, y, core), tensor: 2 (over x).
Axes of the slice: x: 2, y: 2, z: 4, core: 2. Of those that a mesh axis runs over, the one named last changes fastest.
Arguments:
- images: bfloat16 [16, 577, 1024], P('dp'), may hold values from -6 to 6
- cotangent: bfloat16 [16, 577, 1024], P('dp'), may hold values from -6 to 6
- norm1_gain: float32 [1024], replicated, may hold values from 0.5 to 1.5
- norm1_bias: float32 [1024], replicated, may hold values from -3 to 3
- qkv_weight: bfloat16 [1024, 3, 1024], P(None, None, 'tensor'), may hold values from -2 to 2
- qkv_bias: float32 [2, 1024], P(None, 'tensor'), may hold values from -3 to 3
- out_weight: bfloat16 [1024, 1024], P('tensor'), may hold values from -0.5 to 0.5
- out_bias: float32 [1024], replicated, may hold values from -3 to 3
- norm2_gain: float32 [1024], replicated, may hold values from 0.5 to 1.5
- norm2_bias: float32 [1024], replicated, may hold values from -3 to 3
- up_weight: bfloat16 [1024, 4096], P(None, 'tensor'), may hold values from -0.1875 to 0.1875
- up_bias: float32 [4096], P('tensor'), may hold values from -3 to 3
- down_weight: bfloat16 [4096, 1024], P('tensor'), may hold values from -0.09375 to 0.09375
- down_bias: float32 [1024], replicated, may hold values from -3 to 3
Outputs:
- layer_out: bfloat16 [16, 577, 1024], P('dp')
- grad_images: bfloat16 [16, 577, 1024], P('dp')
- grad_norm1_gain: float32 [1024], replicated
- grad_norm1_bias: float32 [1024], replicated
- grad_qkv_weight: float32 [1024, 3, 1024], P(None, None, 'tensor')
- grad_qkv_bias: float32 [2, 1024], P(None, 'tensor')
- grad_out_weight: float32 [1024, 1024], P('tensor')
- grad_out_bias: float32 [1024], replicated
- grad_norm2_gain: float32 [1024], replicated
- grad_norm2_bias: float32 [1024], replicated
- grad_up_weight: float32 [1024, 4096], P(None, 'tensor')
- grad_up_bias: float32 [4096], P('tensor')
- grad_down_weight: float32 [4096, 1024], P('tensor')
- grad_down_bias: float32 [1024], replicated
The draws below stay inside these ranges and needn't reach their ends.
All inputs are finite; a program needn't handle non-finite values.
Results may differ from the reference program's by a relative error of at most 0.03.
Values may be sent and summed in bfloat16 or wider, within the bound.
No kernel may reach another device: no remote copies, remote signals or barrier semaphores. Data moves between devices by JAX's collectives and lax.ppermute only.
A program may use at most 192 MiB of HBM per device.

```python
import jax
import jax.numpy as jnp
from jax import lax

D = 1024
HEADS = 16
HEAD_DIM = 64
FF = 4096
SEQ = 577
IMAGES = 16
N_TENSOR = 2


def draw_qkv_weight(key, part):
    normal_draw = jnp.clip(jax.random.normal(key, (D, 3, D), jnp.float32), -3.0, 3.0) * D ** (-0.5)
    return normal_draw.astype(jnp.bfloat16)


def shard_levels(key, extent, shards, low, largest):
    def one(position, blocks):
        draws = jax.random.uniform(jax.random.fold_in(jax.random.fold_in(key, 6), position), (blocks,), jnp.float32, low / len(shards), largest / len(shards))
        return jnp.repeat(jnp.exp(draws), extent[position] // blocks).reshape((-1,) + (1,) * (len(extent) - position - 1))

    level = one(*shards[0])
    for cut in shards[1:]:
        level = level * one(*cut)
    return level


def scatter_about(rng, dims, spread, limit, cuts=(), dtype=jnp.bfloat16):
    factor_of = shard_levels(rng, dims, cuts, -0.22, 0.18) if cuts else 1.0
    result = jax.random.normal(rng, dims, jnp.float32) * spread * factor_of
    return jnp.minimum(jnp.maximum(result, -limit), limit).astype(dtype)


def setup_inputs(seed: int = 0) -> dict:
    splits = jax.random.split(jax.random.key(seed), 15)
    return {
        "images": scatter_about(splits[0], (IMAGES, SEQ, D), 1.0, 6.0, ((0, 16),)),
        "cotangent": scatter_about(splits[1], (IMAGES, SEQ, D), 1.0, 6.0, ((0, 16),)),
        "norm1_gain": jnp.clip(1.0 + 0.1 * jax.random.normal(splits[2], (D,), jnp.float32), 0.5, 1.5),
        "norm1_bias": scatter_about(splits[3], (D,), 0.5, 3.0, (), jnp.float32),
        "qkv_weight": draw_qkv_weight(jax.random.fold_in(splits[14], 71), 0),
        "qkv_bias": scatter_about(splits[5], (2, D), 0.5, 3.0, ((1, 2),), jnp.float32),
        "out_weight": scatter_about(splits[6], (D, D), (D // 8) ** -0.5, 0.5, ((0, 2),)),
        "out_bias": scatter_about(splits[7], (D,), 0.5, 3.0, (), jnp.float32),
        "norm2_gain": jnp.clip(1.0 + 0.1 * jax.random.normal(splits[8], (D,), jnp.float32), 0.5, 1.5),
        "norm2_bias": scatter_about(splits[9], (D,), 0.5, 3.0, (), jnp.float32),
        "up_weight": scatter_about(splits[10], (D, FF), D ** -0.5, 0.1875, ((1, 2),)),
        "up_bias": scatter_about(splits[11], (FF,), 0.5, 3.0, ((0, 2),), jnp.float32),
        "down_weight": scatter_about(splits[12], (FF, D), FF ** -0.5, 0.09375, ((0, 2),)),
        "down_bias": scatter_about(splits[13], (D,), 0.5, 3.0, (), jnp.float32),
    }


epsilon = 1e-06

def rounded(values):
    return lax.optimization_barrier(values.astype(jnp.bfloat16)).astype(jnp.float32)

def layer_norm(values, gain, bias):
    average = lax.optimization_barrier(jnp.mean(values, axis=-1, keepdims=True))
    centred = values - average
    variance = lax.optimization_barrier(jnp.mean(centred * centred, axis=-1, keepdims=True))
    inv_std = lax.rsqrt(variance + epsilon)
    standard = centred * inv_std
    return (standard * gain + bias, standard, inv_std)

def norm_back(grad_out, standard, inv_std, gain):
    scaled = grad_out * gain
    back = inv_std * (scaled - lax.optimization_barrier(jnp.mean(scaled, axis=-1, keepdims=True)) - standard * lax.optimization_barrier(jnp.mean(scaled * standard, axis=-1, keepdims=True)))
    return (back, lax.optimization_barrier(jnp.sum(grad_out * standard, axis=0)), lax.optimization_barrier(jnp.sum(grad_out, axis=0)))

def gelu_slope(values):
    return 0.5 * (1.0 + jax.scipy.special.erf(values * 0.7071067811865476)) + values * jnp.exp(-0.5 * values * values) * 0.3989422804014327

def reference(images, cotangent, norm1_gain, norm1_bias, qkv_weight, qkv_bias, out_weight, out_bias, norm2_gain, norm2_bias, up_weight, up_bias, down_weight, down_bias):
    score_scale = HEAD_DIM ** (-0.5)
    group_width = D // N_TENSOR
    group_hidden = FF // N_TENSOR
    qkv_float = qkv_weight.astype(jnp.float32)
    out_float = out_weight.astype(jnp.float32)
    up_float = up_weight.astype(jnp.float32)
    down_float = down_weight.astype(jnp.float32)

    def image_step(totals, slices):
        pixels, upstream = slices
        inputs = pixels.astype(jnp.float32)
        normed1, standard1, inv_std1 = layer_norm(inputs, norm1_gain, norm1_bias)
        act1 = normed1.astype(jnp.bfloat16)
        projected = jnp.dot(act1, qkv_weight.reshape(D, 3 * D), preferred_element_type=jnp.float32).reshape(SEQ, 3, D)
        query = (projected[:, 0] + qkv_bias[0]).astype(jnp.bfloat16)
        key_bf = projected[:, 1].astype(jnp.bfloat16)
        value_bf = (projected[:, 2] + qkv_bias[1]).astype(jnp.bfloat16)
        query_heads = query.astype(jnp.float32).reshape(SEQ, HEADS, HEAD_DIM)
        key_heads = key_bf.astype(jnp.float32).reshape(SEQ, HEADS, HEAD_DIM)
        value_heads = value_bf.astype(jnp.float32).reshape(SEQ, HEADS, HEAD_DIM)
        scores = jnp.einsum('qhe,khe->hqk', query_heads, key_heads) * score_scale
        row_peak = lax.optimization_barrier(jnp.max(scores, axis=-1, keepdims=True))
        log_total = row_peak + jnp.log(lax.optimization_barrier(jnp.sum(jnp.exp(scores - row_peak), axis=-1, keepdims=True)))
        prob_exact = jnp.exp(scores - log_total)
        prob_round = rounded(prob_exact)
        attended = jnp.einsum('hqk,khe->qhe', prob_round, value_heads).reshape(SEQ, D).astype(jnp.bfloat16)
        attended_float = attended.astype(jnp.float32)
        attn_parts = jnp.einsum('stc,tcd->tsd', attended_float.reshape(SEQ, N_TENSOR, group_width), out_float.reshape(N_TENSOR, group_width, D))
        attn_total = lax.optimization_barrier(jnp.sum(rounded(attn_parts), axis=0))
        resid = inputs + attn_total + out_bias
        normed2, standard2, inv_std2 = layer_norm(resid, norm2_gain, norm2_bias)
        act2 = normed2.astype(jnp.bfloat16)
        pre_act = jnp.dot(act2, up_weight, preferred_element_type=jnp.float32) + up_bias
        hidden = jax.nn.gelu(pre_act, approximate=False).astype(jnp.bfloat16)
        down_parts = jnp.einsum('stf,tfd->tsd', hidden.astype(jnp.float32).reshape(SEQ, N_TENSOR, group_hidden), down_float.reshape(N_TENSOR, group_hidden, D))
        mlp_total = lax.optimization_barrier(jnp.sum(rounded(down_parts), axis=0))
        layer_out = (resid + mlp_total + down_bias).astype(jnp.bfloat16)
        grad_up = upstream.astype(jnp.float32)
        grad_down_bias = lax.optimization_barrier(jnp.sum(grad_up, axis=0))
        grad_down_weight = jnp.dot(hidden.T, upstream, preferred_element_type=jnp.float32)
        grad_hidden = jnp.dot(upstream, down_weight.T, preferred_element_type=jnp.float32)
        grad_pre = grad_hidden * gelu_slope(pre_act)
        grad_pre_bf = grad_pre.astype(jnp.bfloat16)
        grad_up_bias = lax.optimization_barrier(jnp.sum(grad_pre, axis=0))
        grad_up_weight = jnp.dot(act2.T, grad_pre_bf, preferred_element_type=jnp.float32)
        back_parts = jnp.einsum('stf,dtf->tsd', grad_pre_bf.astype(jnp.float32).reshape(SEQ, N_TENSOR, group_hidden), up_float.reshape(D, N_TENSOR, group_hidden))
        grad_act2 = lax.optimization_barrier(jnp.sum(rounded(back_parts), axis=0))
        back2, grad_norm2_gain, grad_norm2_bias = norm_back(grad_act2, standard2, inv_std2, norm2_gain)
        grad_resid = grad_up + back2
        grad_out_bias = lax.optimization_barrier(jnp.sum(grad_resid, axis=0))
        resid_bf = grad_resid.astype(jnp.bfloat16)
        grad_out_weight = jnp.dot(attended.T, resid_bf, preferred_element_type=jnp.float32)
        grad_att = jnp.dot(resid_bf, out_weight.T, preferred_element_type=jnp.float32).astype(jnp.bfloat16)
        grad_heads = grad_att.astype(jnp.float32).reshape(SEQ, HEADS, HEAD_DIM)
        row_delta = jnp.einsum('qhe,qhe->hq', grad_heads, attended_float.reshape(SEQ, HEADS, HEAD_DIM))
        grad_prob = jnp.einsum('qhe,khe->hqk', grad_heads, value_heads)
        score_round = rounded(prob_exact * (grad_prob - row_delta[:, :, None]))
        grad_query = jnp.einsum('hqk,khe->qhe', score_round, key_heads).reshape(SEQ, D) * score_scale
        grad_key = jnp.einsum('hqk,qhe->khe', score_round, query_heads).reshape(SEQ, D) * score_scale
        grad_value = jnp.einsum('hqk,qhe->khe', prob_round, grad_heads).reshape(SEQ, D)
        grad_proj = jnp.stack([grad_query, grad_key, grad_value], axis=1).astype(jnp.bfloat16)
        grad_qkv_bias = jnp.stack([lax.optimization_barrier(jnp.sum(grad_query, axis=0)), lax.optimization_barrier(jnp.sum(grad_value, axis=0))], axis=0)
        grad_qkv_weight = jnp.dot(act1.T, grad_proj.reshape(SEQ, 3 * D), preferred_element_type=jnp.float32).reshape(D, 3, D)
        back1_parts = jnp.einsum('sgtc,dgtc->tsd', grad_proj.astype(jnp.float32).reshape(SEQ, 3, N_TENSOR, group_width), qkv_float.reshape(D, 3, N_TENSOR, group_width))
        grad_act1 = lax.optimization_barrier(jnp.sum(rounded(back1_parts), axis=0))
        back1, grad_norm1_gain, grad_norm1_bias = norm_back(grad_act1, standard1, inv_std1, norm1_gain)
        grad_images = (grad_resid + back1).astype(jnp.bfloat16)
        fresh = (grad_norm1_gain, grad_norm1_bias, grad_qkv_weight, grad_qkv_bias, grad_out_weight, grad_out_bias, grad_norm2_gain, grad_norm2_bias, grad_up_weight, grad_up_bias, grad_down_weight, grad_down_bias)
        totals = tuple((older + newer for older, newer in zip(totals, fresh)))
        return (totals, (layer_out, grad_images))
    zeros_init = (jnp.zeros((D,), jnp.float32), jnp.zeros((D,), jnp.float32), jnp.zeros((D, 3, D), jnp.float32), jnp.zeros((2, D), jnp.float32), jnp.zeros((D, D), jnp.float32), jnp.zeros((D,), jnp.float32), jnp.zeros((D,), jnp.float32), jnp.zeros((D,), jnp.float32), jnp.zeros((D, FF), jnp.float32), jnp.zeros((FF,), jnp.float32), jnp.zeros((FF, D), jnp.float32), jnp.zeros((D,), jnp.float32))
    totals, outputs = lax.scan(image_step, zeros_init, (images, cotangent))
    layer_out, grad_images = outputs
    return (layer_out, grad_images, totals[0], totals[1], totals[2], totals[3], totals[4], totals[5], totals[6], totals[7], totals[8], totals[9], totals[10], totals[11])
```

```python
import functools

import jax
import jax.numpy as jnp
from jax import lax
from jax.experimental import pallas as pl
from jax.experimental.pallas import tpu as pltpu
from jax.sharding import PartitionSpec as P

HEAD_DIM = 64
EPSILON = 1e-06
F32 = jnp.float32
BF16 = jnp.bfloat16


def layer_norm(values, gain, bias):
    average = jnp.mean(values, axis=-1, keepdims=True)
    centred = values - average
    variance = jnp.mean(centred * centred, axis=-1, keepdims=True)
    inv_std = lax.rsqrt(variance + EPSILON)
    standard = centred * inv_std
    return (standard * gain + bias, standard, inv_std)


def norm_back(grad_out, standard, inv_std, gain):
    scaled = grad_out * gain
    back = inv_std * (
        scaled
        - jnp.mean(scaled, axis=-1, keepdims=True)
        - standard * jnp.mean(scaled * standard, axis=-1, keepdims=True)
    )
    return (back, jnp.sum(grad_out * standard, axis=0), jnp.sum(grad_out, axis=0))


def gelu_slope(values):
    return (
        0.5 * (1.0 + jax.scipy.special.erf(values * 0.7071067811865476))
        + values * jnp.exp(-0.5 * values * values) * 0.3989422804014327
    )


class Group:
    def __init__(self, size):
        self.size = size
        self.n = size.bit_length() - 1
        assert 1 << self.n == size and self.n >= 4
        self.me = lax.axis_index("dp")
        self.z1 = 1 << (self.n - 2)
        self.z2 = 3 << (self.n - 2)
        self.mid = [1 << b for b in range(1, self.n - 2)]

    def swap(self, value, mask):
        return lax.ppermute(value, "dp", [(i, i ^ mask) for i in range(self.size)])

    def bit(self, mask):
        if mask == self.z1:
            return ((self.me >> (self.n - 2)) ^ (self.me >> (self.n - 1))) & 1
        return (self.me // mask) & 1


def rows_of(value, start, size):
    return lax.dynamic_slice_in_dim(value, start, size, 0)


def assemble_kernel(me_ref, own_ref, other_ref, out_ref, *, half):
    relative = jnp.bitwise_xor(pl.program_id(0), me_ref[0])

    @pl.when(relative < half)
    def _():
        out_ref[...] = own_ref[...].astype(F32)

    @pl.when(relative >= half)
    def _():
        out_ref[...] = other_ref[...].astype(F32)


def assemble(own, other, me, blocks):
    half = blocks // 2
    rows, width = own.shape[0] // half, own.shape[1]

    def own_map(i, me_ref):
        relative = jnp.bitwise_xor(i, me_ref[0])
        return (jnp.where(relative < half, relative, half - 1), 0)

    def other_map(i, me_ref):
        relative = jnp.bitwise_xor(i, me_ref[0])
        return (jnp.where(relative >= half, relative - half, 0), 0)

    return pl.pallas_call(
        functools.partial(assemble_kernel, half=half),
        out_shape=jax.ShapeDtypeStruct((rows * blocks, width), F32),
        grid_spec=pltpu.PrefetchScalarGridSpec(
            num_scalar_prefetch=1,
            grid=(blocks,),
            in_specs=[pl.BlockSpec((rows, width), own_map), pl.BlockSpec((rows, width), other_map)],
            out_specs=pl.BlockSpec((rows, width), lambda i, me_ref: (i, 0)),
        ),
        cost_estimate=pl.CostEstimate(
            flops=0, transcendentals=0, bytes_accessed=rows * blocks * width * 6
        ),
        name="assemble",
    )(me.reshape(1), own, other)


def reduce_rows(group, make, rows, masks):
    count = len(masks)
    bits = [group.bit(mask) for mask in masks]
    half = rows // 2
    got = group.swap(make((1 - bits[0]) * half, half).astype(BF16), masks[0])
    start = bits[0] * half
    quarter = half // 2
    away, keep = (1 - bits[1]) * quarter, bits[1] * quarter
    sent = make(start + away, quarter) + rows_of(got, away, quarter).astype(F32)
    got_next = group.swap(sent.astype(BF16), masks[1])
    held = make(start + keep, quarter) + rows_of(got, keep, quarter).astype(F32)
    got, size = got_next, quarter
    for level in range(2, count):
        size //= 2
        away, keep = (1 - bits[level]) * size, bits[level] * size
        sent = rows_of(held, away, size) + rows_of(got, away, size).astype(F32)
        got_next = group.swap(sent.astype(BF16), masks[level])
        held = rows_of(held, keep, size) + rows_of(got, keep, size).astype(F32)
        got = got_next
    total = (held + got.astype(F32)).astype(BF16)
    total = (total.astype(F32) + group.swap(total, group.z2).astype(F32)).astype(BF16)
    for level in range(count - 1, 0, -1):
        total = jnp.concatenate([total, group.swap(total, masks[level])], axis=0)
    other = group.swap(total, masks[0])
    index = sum(bit << (count - 1 - level) for level, bit in enumerate(bits))
    return assemble(total, other, index.astype(jnp.int32), 1 << count)


def reduce_small(group, value):
    for mask in [1] + group.mid + [group.z1, group.z2]:
        value = value + group.swap(value, mask)
    return value


def on_device(
    images,
    cotangent,
    norm1_gain,
    norm1_bias,
    qkv_weight,
    qkv_bias,
    out_weight,
    out_bias,
    norm2_gain,
    norm2_bias,
    up_weight,
    up_bias,
    down_weight,
    down_bias,
    *,
    dp,
    tensor,
):
    assert tensor == 2
    group = Group(dp)
    side = lax.axis_index("tensor")

    def across(value):
        return lax.ppermute(value, "tensor", [(0, 1), (1, 0)])

    def both(value, axis):
        other = across(value)
        low, high = jnp.where(side == 0, value, other), jnp.where(side == 0, other, value)
        return jnp.concatenate([low, high], axis=axis)

    num_images, seq_length, width = images.shape
    tok_rows = num_images * seq_length
    local_cols = qkv_weight.shape[2]
    local_heads = local_cols // HEAD_DIM
    score_scale = HEAD_DIM ** (-0.5)
    out_whole = both(out_weight, 0)
    inputs = images.reshape(tok_rows, width).astype(F32)
    upstream = cotangent.reshape(tok_rows, width)
    grad_up = upstream.astype(F32)
    normed1, standard1, inv_std1 = layer_norm(inputs, norm1_gain, norm1_bias)
    act1 = normed1.astype(BF16)
    planes = jnp.transpose(qkv_weight, (1, 0, 2))
    head_shape = (num_images, seq_length, local_heads, HEAD_DIM)

    def project(index):
        return jnp.dot(act1, planes[index], preferred_element_type=F32)

    query_heads = (project(0) + qkv_bias[0]).astype(BF16).reshape(head_shape)
    key_heads = project(1).astype(BF16).reshape(head_shape)
    value_heads = (project(2) + qkv_bias[1]).astype(BF16).reshape(head_shape)
    scores = (
        jnp.einsum("ishe,ikhe->ihsk", query_heads, key_heads, preferred_element_type=F32)
        * score_scale
    )
    row_peak = jnp.max(scores, axis=-1, keepdims=True)
    log_total = row_peak + jnp.log(jnp.sum(jnp.exp(scores - row_peak), axis=-1, keepdims=True))
    prob_bf = jnp.exp(scores - log_total).astype(BF16)
    attended_heads = jnp.einsum(
        "ihsk,ikhe->ishe", prob_bf, value_heads, preferred_element_type=F32
    ).astype(BF16)
    attended = attended_heads.reshape(tok_rows, local_cols)
    attn_total = jnp.dot(both(attended, 1), out_whole, preferred_element_type=F32)
    grad_hidden = jnp.einsum("rd,fd->rf", upstream, down_weight, preferred_element_type=F32)
    grad_down_bias = jnp.sum(grad_up, axis=0)
    resid = inputs + attn_total + out_bias
    normed2, standard2, inv_std2 = layer_norm(resid, norm2_gain, norm2_bias)
    act2 = normed2.astype(BF16)
    pre_act = jnp.dot(act2, up_weight, preferred_element_type=F32) + up_bias
    hidden = jax.nn.gelu(pre_act, approximate=False).astype(BF16)
    grad_pre = grad_hidden * gelu_slope(pre_act)
    grad_pre_bf = grad_pre.astype(BF16)
    grad_up_bias = jnp.sum(grad_pre, axis=0)
    back_term = jnp.einsum("rf,df->rd", grad_pre_bf, up_weight, preferred_element_type=F32).astype(BF16)
    back_other = across(back_term)

    def weight_rows(left, right):
        def make(start, size):
            part = lax.dynamic_slice_in_dim(left, start, size, 1)
            return jnp.einsum("rf,rd->fd", part, right, preferred_element_type=F32)

        return make

    order_p = [1] + group.mid + [group.z1]
    order_q = [1, group.z1] + group.mid
    grad_down_weight = reduce_rows(group, weight_rows(hidden, upstream), hidden.shape[1], order_p)
    grad_up_weight = reduce_rows(group, weight_rows(act2, grad_pre_bf), width, order_q)

    down_term = jnp.dot(hidden, down_weight, preferred_element_type=F32).astype(BF16)
    mlp_total = down_term.astype(F32) + across(down_term).astype(F32)
    layer_out = (resid + mlp_total + down_bias).astype(BF16).reshape(images.shape)

    grad_act2 = back_term.astype(F32) + back_other.astype(F32)
    back2, grad_norm2_gain, grad_norm2_bias = norm_back(grad_act2, standard2, inv_std2, norm2_gain)
    grad_resid = grad_up + back2
    grad_out_bias = jnp.sum(grad_resid, axis=0)
    resid_bf = grad_resid.astype(BF16)
    grad_out_weight = reduce_rows(group, weight_rows(attended, resid_bf), local_cols, order_p)
    grad_att = jnp.einsum("rd,cd->rc", resid_bf, out_weight, preferred_element_type=F32).astype(BF16)
    grad_heads = grad_att.reshape(head_shape)
    again = (
        jnp.einsum("ishe,ikhe->ihsk", query_heads, key_heads, preferred_element_type=F32)
        * score_scale
    )
    prob_exact = jnp.exp(again - log_total)
    prob_again = prob_exact.astype(BF16)
    row_delta = jnp.einsum(
        "ishe,ishe->ihs", grad_heads, attended_heads, preferred_element_type=F32
    )
    grad_prob = jnp.einsum("ishe,ikhe->ihsk", grad_heads, value_heads, preferred_element_type=F32)
    score_bf = (prob_exact * (grad_prob - row_delta[..., None])).astype(BF16)
    grad_query = (
        jnp.einsum("ihsk,ikhe->ishe", score_bf, key_heads, preferred_element_type=F32).reshape(
            tok_rows, local_cols
        )
        * score_scale
    )
    grad_key = (
        jnp.einsum("ihsk,ishe->ikhe", score_bf, query_heads, preferred_element_type=F32).reshape(
            tok_rows, local_cols
        )
        * score_scale
    )
    grad_value = jnp.einsum(
        "ihsk,ishe->ikhe", prob_again, grad_heads, preferred_element_type=F32
    ).reshape(tok_rows, local_cols)
    grad_qkv_bias = jnp.stack([jnp.sum(grad_query, axis=0), jnp.sum(grad_value, axis=0)], axis=0)
    grad_proj = jnp.concatenate(
        [grad_query.astype(BF16), grad_key.astype(BF16), grad_value.astype(BF16)], axis=1
    )
    qkv_rows = reduce_rows(group, weight_rows(act1, grad_proj), width, order_p)
    grad_qkv_weight = qkv_rows.reshape(width, 3, local_cols)
    back1_term = sum(
        jnp.einsum(
            "rc,dc->rd",
            grad_proj[:, index * local_cols : (index + 1) * local_cols],
            planes[index],
            preferred_element_type=F32,
        )
        for index in range(3)
    ).astype(BF16)
    grad_act1 = back1_term.astype(F32) + across(back1_term).astype(F32)
    back1, grad_norm1_gain, grad_norm1_bias = norm_back(grad_act1, standard1, inv_std1, norm1_gain)
    grad_images = (grad_resid + back1).astype(BF16).reshape(images.shape)
    small = [
        grad_norm1_gain,
        grad_norm1_bias,
        grad_qkv_bias,
        grad_out_bias,
        grad_norm2_gain,
        grad_norm2_bias,
        grad_up_bias,
        grad_down_bias,
    ]
    packed = jnp.concatenate([value.reshape(-1) for value in small])
    summed = reduce_small(group, packed.reshape(-1, 128)).reshape(-1)
    outs, start = [], 0
    for value in small:
        outs.append(summed[start : start + value.size].reshape(value.shape))
        start += value.size
    return (
        layer_out,
        grad_images,
        outs[0],
        outs[1],
        grad_qkv_weight,
        outs[2],
        grad_out_weight,
        outs[3],
        outs[4],
        outs[5],
        grad_up_weight,
        outs[6],
        grad_down_weight,
        outs[7],
    )


def solution(mesh):
    in_specs = (
        P("dp", None, None),
        P("dp", None, None),
        P(),
        P(),
        P(None, None, "tensor"),
        P(None, "tensor"),
        P("tensor", None),
        P(),
        P(),
        P(),
        P(None, "tensor"),
        P("tensor"),
        P("tensor", None),
        P(),
    )
    out_specs = (
        P("dp", None, None),
        P("dp", None, None),
        P(),
        P(),
        P(None, None, "tensor"),
        P(None, "tensor"),
        P("tensor", None),
        P(),
        P(),
        P(),
        P(None, "tensor"),
        P("tensor"),
        P("tensor", None),
        P(),
    )
    body = functools.partial(on_device, dp=mesh.shape["dp"], tensor=mesh.shape["tensor"])
    return jax.shard_map(body, mesh=mesh, in_specs=in_specs, out_specs=out_specs, check_vma=False)
```
